32 devices in a mesh: src: 4 (over x, core), dst: 2 (over y), tm: 4 (over z).
Axes of the slice: x: 2, y: 2, z: 4, core: 2. Of those that a mesh axis runs over, the one named last changes fastest.
Arguments:
- traffic: bfloat16 [256, 256, 512], P('src', 'dst', 'tm'), may hold values from -6 to 6
- src_factor: float32 [256, 64], P('src'), may hold values from -0.75 to 0.75
- dst_factor: float32 [256, 64], P('dst'), may hold values from -0.75 to 0.75
- time_factor: float32 [512, 64], P('tm'), may hold values from -0.75 to 0.75
Outputs:
- grad_src: float32 [256, 64], P('src')
- grad_dst: float32 [256, 64], P('dst')
- grad_time: float32 [512, 64], P('tm')
The draws below stay inside these ranges and needn't reach their ends.
All inputs are finite; a program needn't handle non-finite values.
Results may differ from the reference program's by a relative error of at most 0.0003.
Values sent between devices are 32-bit elements; how exact they have to be, the bound alone decides.
No kernel may reach another device: no remote copies, remote signals or barrier semaphores. Data moves between devices by JAX's collectives and lax.ppermute only.
A program may use at most 64 MiB of HBM per device.

```python
import jax
import jax.numpy as jnp
from jax import lax

I_DEV = 64
R = 64
DAY = 288
STEPS = 3
NI = 256
NJ = 256
NK = 512


def spiked(result, key, source, target, shards_of, factor):
    def block_of(axis_at):
        return (jnp.arange(result.shape[axis_at]) // (result.shape[axis_at] // shards_of)).reshape((-1,) + (1,) * (result.ndim - 1 - axis_at))

    first = jax.random.permutation(key, shards_of)[block_of(target)]
    far = (block_of(target) + shards_of // 2) % shards_of
    return jnp.where((block_of(source) == first) | (block_of(source) == far), factor * result, result)


def steps_of(own_key, extent, cuts, smallest, largest):
    level, own = 1.0, jax.random.fold_in(own_key, 6)
    for position, parts in cuts:
        draws = jnp.exp(jax.random.uniform(jax.random.fold_in(own, position), (parts,), jnp.float32, smallest / len(cuts), largest / len(cuts)))
        level = level * jnp.repeat(draws, extent[position] // parts).reshape([-1 if axis == position else 1 for axis in range(len(extent))])
    return level


def gaussian(key, dims, deviation, reach, split=(), dtype=jnp.bfloat16):
    entries = jax.random.normal(key, dims, jnp.float32) * deviation
    if len(split) > 0:
        entries = steps_of(key, dims, split, -0.22, 0.18) * entries
    return jnp.clip(entries, min=-reach, max=reach).astype(dtype)


def bell_draw_with(rng, shape, width, reach, shards, heavy, dtype=jnp.bfloat16):
    drawn = width * jax.random.normal(rng, shape, jnp.float32)
    if shards:
        drawn = drawn * steps_of(rng, shape, shards, -0.22, 0.18)
    return jnp.clip(spiked(drawn, jax.random.fold_in(rng, 3), *heavy), -reach, reach).astype(dtype)


def setup_inputs(seed: int = 0) -> dict:
    seeds = jax.random.split(jax.random.key(seed), 5)
    return {
        "traffic": bell_draw_with(seeds[0], (NI, NJ, NK), 1.0, 6.0, ((0, 4), (1, 2), (2, 4)), (0, 2, 4, 2.0)),
        "src_factor": gaussian(seeds[1], (NI, R), R ** -0.5, 0.75, ((0, 4),), jnp.float32),
        "dst_factor": gaussian(seeds[2], (NJ, R), R ** -0.5, 0.75, ((0, 2),), jnp.float32),
        "time_factor": gaussian(seeds[3], (NK, R), R ** -0.5, 0.75, ((0, 4),), jnp.float32),
    }


hour_weight = 32.0
day_weight = 64.0
step_rate = 0.1
highest = lax.Precision.HIGHEST


def smoothing(time_now):
    rank_count = time_now.shape[1]
    zero_one = jnp.zeros((1, rank_count), jnp.float32)
    zero_day = jnp.zeros((DAY, rank_count), jnp.float32)
    hour_diff = jnp.concatenate([zero_one, time_now[1:] - time_now[:-1]], 0)
    day_diff = jnp.concatenate([zero_day, time_now[DAY:] - time_now[:-DAY]], 0)
    hour_next = jnp.concatenate([hour_diff[1:], zero_one], 0)
    day_next = jnp.concatenate([day_diff[DAY:], zero_day], 0)
    return hour_weight * (hour_diff - hour_next) + day_weight * (day_diff - day_next)


def evaluate(traffic, src_now, dst_now, time_now):
    dst_total = dst_now.shape[0]
    time_total = time_now.shape[0]
    rank_count = src_now.shape[1]
    dst_time = (dst_now.T[:, :, None] * time_now.T[:, None, :]).reshape(rank_count, dst_total * time_total)
    blocks = traffic.reshape(-1, I_DEV, dst_total * time_total)
    src_blocks = src_now.reshape(-1, I_DEV, rank_count)

    def visit(carried, scanned):
        dst_sum, time_sum = carried
        observed, src_rows = scanned
        model_cells = jnp.dot(src_rows, dst_time, precision=highest)
        residual = model_cells - observed.astype(jnp.float32)
        raw_src = jnp.einsum("ix,rx->ir", residual, dst_time, precision=highest)
        resid_cube = residual.reshape(I_DEV, dst_total, time_total)
        src_time = src_rows.T[:, :, None] * time_now.T[:, None, :]
        src_dst = src_rows.T[:, :, None] * dst_now.T[:, None, :]
        dst_sum = dst_sum + jnp.einsum("ijk,rik->jr", resid_cube, src_time, precision=highest)
        time_sum = time_sum + jnp.einsum("ijk,rij->kr", resid_cube, src_dst, precision=highest)
        return (dst_sum, time_sum), raw_src

    initial = (jnp.zeros((dst_total, rank_count), jnp.float32), jnp.zeros((time_total, rank_count), jnp.float32))
    (raw_dst, raw_time), raw_src = lax.scan(visit, initial, (blocks, src_blocks))
    grad_src = raw_src.reshape(-1, rank_count) / rank_count
    grad_dst = raw_dst / rank_count
    grad_time = (raw_time + smoothing(time_now)) / rank_count
    return grad_src, grad_dst, grad_time


def reference(traffic, src_factor, dst_factor, time_factor):
    src_now, dst_now, time_now = src_factor, dst_factor, time_factor
    grad_src, grad_dst, grad_time = evaluate(traffic, src_now, dst_now, time_now)
    for iteration in range(STEPS - 1):
        src_now = src_now - step_rate * grad_src
        dst_now = dst_now - step_rate * grad_dst
        time_now = time_now - step_rate * grad_time
        grad_src, grad_dst, grad_time = evaluate(traffic, src_now, dst_now, time_now)
    return grad_src, grad_dst, grad_time
```

```python
import functools

import jax
import jax.numpy as jnp
from jax import lax
from jax.experimental import pallas as pl
from jax.experimental.pallas import tpu as pltpu
from jax.sharding import PartitionSpec as P

DAY = 288
STEPS = 3

hour_weight = 32.0
day_weight = 64.0
step_rate = 0.1
highest = lax.Precision.HIGHEST
f32 = jnp.float32
bf16 = jnp.bfloat16
LANES = 128
AXES = ("src", "dst", "tm")
BY_LANES = (((1,), (1,)), ((), ()))
VMEM = pl.BlockSpec(memory_space=pltpu.VMEM)
PARAMS = pltpu.CompilerParams(vmem_limit_bytes=24 << 20)


def halves(x):
    high = x.astype(bf16)
    low = (x - high.astype(f32)).astype(bf16)
    return jnp.concatenate([high, low], 0)


def gram(x):
    return lax.dot_general(x, x, BY_LANES, precision=highest, preferred_element_type=f32)


def times(a, b):
    return jnp.dot(a, b, precision=highest, preferred_element_type=f32)


def packed(x):
    fold = LANES // x.shape[1] if x.shape[1] < LANES else 1
    rows = x.shape[0] // fold
    return x if fold == 1 else jnp.concatenate([x[i * rows : (i + 1) * rows] for i in range(fold)], 1)


def unpacked(x, columns):
    fold = x.shape[1] // columns
    return x if fold == 1 else jnp.concatenate([x[:, i * columns : (i + 1) * columns] for i in range(fold)], 0)


def src_dst_kernel(slice_rows, traffic, src, dst, time, out):
    src_now, dst_now, time_now = src[...], dst[...], time[...]
    rank, src_rows = src_now.shape
    dst_rows, time_rows = dst_now.shape[1], time_now.shape[1]
    time_halves = halves(time_now)
    dst_wide = jnp.concatenate([dst_now, dst_now], 0).T
    src_wide = jnp.concatenate([src_now, src_now], 0).T
    dst_sum = jnp.zeros((dst_rows, 2 * rank), f32)
    rows = []
    step = 4
    for first in range(0, src_rows, step):
        block = traffic[first : first + step].reshape(step * dst_rows, time_rows)
        seen = lax.dot_general(block, time_halves, BY_LANES, preferred_element_type=f32)
        for i in range(step):
            part = seen[i * dst_rows : (i + 1) * dst_rows]
            dst_sum = dst_sum + part * src_wide[first + i : first + i + 1]
            rows.append(jnp.sum(part * dst_wide, axis=0, keepdims=True))
    src_sum = jnp.concatenate(rows, 0)
    src_seen = (src_sum[:, :rank] + src_sum[:, rank:]).T
    dst_seen = (dst_sum[:, :rank] + dst_sum[:, rank:]).T
    time_gram = gram(time_now)
    src_part = times(gram(dst_now) * time_gram, src_now) - src_seen
    dst_part = times(gram(src_now) * time_gram, dst_now) - dst_seen
    src_packed = packed(src_part)
    top = src_packed.shape[0]
    out[:top] = src_packed
    out[top : top + rank] = dst_part
    place = lax.axis_index("src") * lax.axis_size("dst") + lax.axis_index("dst")
    place = jnp.minimum(place, rank // slice_rows - 1)
    out[top + rank :] = time[pl.ds(pl.multiple_of(place * slice_rows, slice_rows), slice_rows)]


def time_kernel(traffic, src, dst, time, out):
    src_now, dst_now, time_now = src[...], dst[...], time[...]
    rank, src_rows = src_now.shape
    dst_halves = halves(dst_now)
    total = times(gram(src_now) * gram(dst_now), time_now)
    seen_sum = jnp.zeros(total.shape, f32)
    for i in range(src_rows):
        seen = jnp.dot(dst_halves, traffic[i], preferred_element_type=f32)
        seen_sum = seen_sum + (seen[:rank] + seen[rank:]) * src_now[:, i : i + 1]
    out[...] = total - seen_sum


def back(x, offset, position):
    if offset >= x.shape[1]:
        return jnp.zeros_like(x)
    return jnp.where(position >= offset, pltpu.roll(x, offset, 1), 0.0)


def forth(x, offset, position):
    size = x.shape[1]
    if offset >= size:
        return jnp.zeros_like(x)
    return jnp.where(position < size - offset, pltpu.roll(x, size - offset, 1), 0.0)


def smooth_kernel(slice_rows, src_top, blocks, *refs):
    held, time_part, src_out, both_out = refs[:blocks], refs[blocks], refs[-2], refs[-1]
    rank, time_rows = time_part.shape
    here = lax.axis_index("tm")
    total = held[0][: src_top + rank]
    for other in held[1:]:
        total = total + other[: src_top + rank]
    src_out[...] = total[:src_top]
    both_out[:rank] = total[src_top:]
    slices = [h[src_top + rank :] for h in held]
    ordered = []
    for block in range(blocks):
        pick = slices[0]
        for mask in range(1, blocks):
            pick = jnp.where((here ^ block) == mask, slices[mask], pick)
        ordered.append(pick)
    whole = jnp.concatenate(ordered, 1)
    position = lax.broadcasted_iota(jnp.int32, whole.shape, 1)
    hour_diff = jnp.where(position >= 1, whole - back(whole, 1, position), 0.0)
    day_diff = jnp.where(position >= DAY, whole - back(whole, DAY, position), 0.0)
    smooth = hour_weight * (hour_diff - forth(hour_diff, 1, position))
    smooth = smooth + day_weight * (day_diff - forth(day_diff, DAY, position))
    mine = smooth[:, :time_rows]
    for block in range(1, blocks):
        mine = jnp.where(here == block, smooth[:, block * time_rows : (block + 1) * time_rows], mine)
    both_out[rank:] = time_part[...]
    place = lax.axis_index("src") * lax.axis_size("dst") + lax.axis_index("dst")
    count = rank // slice_rows
    mine = jnp.where(place < count, mine, 0.0)
    start = pl.multiple_of(rank + jnp.minimum(place, count - 1) * slice_rows, slice_rows)
    both_out[pl.ds(start, slice_rows)] = both_out[pl.ds(start, slice_rows)] + mine


def exchanged(x, src_mask, dst_mask, tm_mask):
    src_size, dst_size, tm_size = (lax.axis_size(a) for a in AXES)
    route = []
    for s in range(src_size):
        for d in range(dst_size):
            for t in range(tm_size):
                here = (s * dst_size + d) * tm_size + t
                there = ((s ^ src_mask) * dst_size + (d ^ dst_mask)) * tm_size + (t ^ tm_mask)
                route.append((here, there))
    return lax.ppermute(x, AXES, route)


def on_device(traffic, src_factor, dst_factor, time_factor):
    src_rows, rank = src_factor.shape
    src_size, dst_size, tm_size = (lax.axis_size(a) for a in AXES)
    slice_rows = max(8, rank // (src_size * dst_size))
    src_now, dst_now, time_now = src_factor.T, dst_factor.T, time_factor.T
    dst_rows, time_rows = dst_now.shape[1], time_now.shape[1]
    src_top = rank * src_rows // LANES if src_rows < LANES else rank
    first_kernel = pl.pallas_call(
        functools.partial(src_dst_kernel, slice_rows),
        out_shape=jax.ShapeDtypeStruct((src_top + rank + slice_rows, LANES), f32),
        in_specs=[VMEM] * 4,
        out_specs=VMEM,
        compiler_params=PARAMS,
        name="src_dst_part",
    )
    second_kernel = pl.pallas_call(
        time_kernel,
        out_shape=jax.ShapeDtypeStruct((rank, time_rows), f32),
        in_specs=[VMEM] * 4,
        out_specs=VMEM,
        compiler_params=PARAMS,
        name="time_part",
    )
    third_kernel = pl.pallas_call(
        functools.partial(smooth_kernel, slice_rows, src_top, tm_size),
        out_shape=(
            jax.ShapeDtypeStruct((src_top, LANES), f32),
            jax.ShapeDtypeStruct((2 * rank, time_rows), f32),
        ),
        in_specs=[VMEM] * (tm_size + 1),
        out_specs=(VMEM, VMEM),
        compiler_params=PARAMS,
        name="tm_sums",
    )
    for iteration in range(STEPS):
        mixed = first_kernel(traffic, src_now, dst_now, time_now)
        others = [exchanged(mixed, 0, 0, mask) for mask in range(1, tm_size)]
        time_part = second_kernel(traffic, src_now, dst_now, time_now)
        src_sum, both = third_kernel(mixed, *others, time_part)
        if src_size > 1:
            both = both + exchanged(both, 1, 0, 0)
        src_mask, dst_mask = 2, 1
        while src_mask < src_size or dst_mask < dst_size:
            add_both, add_src, add_time = jnp.zeros_like(both), jnp.zeros_like(src_sum), 0.0
            if src_mask < src_size:
                add_both = exchanged(both, src_mask, 0, 0)
            if dst_mask < dst_size:
                stacked = jnp.concatenate([src_sum, both[rank:]], 0)
                add_y = exchanged(stacked, 0, dst_mask, 0)
                add_src, add_time = add_y[:src_top], add_y[src_top:]
            if src_mask < src_size and dst_mask < dst_size:
                add_time = add_time + exchanged(both[rank:], src_mask, dst_mask, 0)
            src_sum = src_sum + add_src
            both = jnp.concatenate(
                [both[:rank] + add_both[:rank], both[rank:] + add_both[rank:] + add_time], 0
            )
            src_mask, dst_mask = src_mask * 2, dst_mask * 2
        grad_src = unpacked(src_sum, src_rows) / rank
        grad_dst = both[:rank] / rank
        grad_time = both[rank:] / rank
        if iteration + 1 < STEPS:
            src_now = src_now - step_rate * grad_src
            dst_now = dst_now - step_rate * grad_dst
            time_now = time_now - step_rate * grad_time
    return (grad_src.T, grad_dst.T, grad_time.T)


def solution(mesh):
    in_specs = (P("src", "dst", "tm"), P("src", None), P("dst", None), P("tm", None))
    out_specs = (P("src", None), P("dst", None), P("tm", None))
    return jax.shard_map(
        on_device, mesh=mesh, in_specs=in_specs, out_specs=out_specs, check_vma=False
    )
```

```python
import functools

import jax
import jax.numpy as jnp
from jax import lax
from jax.experimental import pallas as pl
from jax.experimental.pallas import tpu as pltpu
from jax.sharding import PartitionSpec as P


DAY = 288
STEPS = 3

hour_weight = 32.0
day_weight = 64.0
step_rate = 0.1
highest = lax.Precision.HIGHEST
f32 = jnp.float32
bf16 = jnp.bfloat16
LANES = 128
AXES = ("src", "dst", "tm")
BY_LANES = (((1,), (1,)), ((), ()))
VMEM = pl.BlockSpec(memory_space=pltpu.VMEM)
PARAMS = pltpu.CompilerParams(vmem_limit_bytes=24 << 20)


def halves(x):
    high = x.astype(bf16)
    low = (x - high.astype(f32)).astype(bf16)
    return jnp.concatenate([high, low], 0)


def gram(x):
    return lax.dot_general(x, x, BY_LANES, precision=highest, preferred_element_type=f32)


def times(a, b):
    return jnp.dot(a, b, precision=highest, preferred_element_type=f32)


def packed(x):
    fold = LANES // x.shape[1] if x.shape[1] < LANES else 1
    rows = x.shape[0] // fold
    return x if fold == 1 else jnp.concatenate([x[i * rows : (i + 1) * rows] for i in range(fold)], 1)


def unpacked(x, columns):
    fold = x.shape[1] // columns
    return x if fold == 1 else jnp.concatenate([x[:, i * columns : (i + 1) * columns] for i in range(fold)], 0)


def place_of(count):
    place = lax.axis_index("src") * (lax.axis_size("dst") // 2) + lax.axis_index("dst") // 2
    return jnp.minimum(place, count - 1), place < count


def src_dst_part(slice_rows, traffic, src_now, dst_now, time_now, time, out, ready=None):
    rank = src_now.shape[1]
    src_rows, dst_rows, time_rows = traffic.shape
    time_halves = halves(time_now)
    dst_wide = jnp.concatenate([dst_now, dst_now], 0).T
    src_wide = jnp.concatenate([src_now, src_now], 1)
    dst_sum = jnp.zeros((dst_rows, 2 * rank), f32)
    rows = []
    step = 4
    for first in range(0, src_rows, step):
        if ready is not None:
            ready(first)
        block = traffic[first : first + step].reshape(step * dst_rows, time_rows)
        seen = lax.dot_general(block, time_halves, BY_LANES, preferred_element_type=f32)
        for i in range(step):
            part = seen[i * dst_rows : (i + 1) * dst_rows]
            dst_sum = dst_sum + part * src_wide[first + i : first + i + 1]
            rows.append(jnp.sum(part * dst_wide, axis=0, keepdims=True))
    src_sum = jnp.concatenate(rows, 0)
    dst_seen = (dst_sum[:, :rank] + dst_sum[:, rank:]).T
    time_gram = gram(time_now)
    src_part = times(src_now, gram(dst_now) * time_gram) - (src_sum[:, :rank] + src_sum[:, rank:])
    dst_part = times(gram(src_now.T) * time_gram, dst_now) - dst_seen
    src_packed = packed(src_part)
    top = src_packed.shape[0]
    out[:top] = src_packed
    out[top : top + rank] = dst_part
    start = pl.multiple_of(place_of(rank // slice_rows)[0] * slice_rows, slice_rows)
    out[top + rank :] = time[pl.ds(start, slice_rows)]


def src_dst_kernel(slice_rows, traffic, src, dst, time, out):
    src_dst_part(slice_rows, traffic, src[...], dst[...], time[...], time, out)


def entry_kernel(slice_rows, traffic_in, src_in, dst_in, time_in, out, traffic, src, dst, time, arrived):
    chunks = arrived.shape[0] - 3
    chunk = traffic.shape[0] // chunks
    small = [
        pltpu.make_async_copy(a, b, arrived.at[chunks + i])
        for i, (a, b) in enumerate(((src_in, src), (dst_in, dst), (time_in, time)))
    ]
    large = [
        pltpu.make_async_copy(
            traffic_in.at[pl.ds(i * chunk, chunk)], traffic.at[pl.ds(i * chunk, chunk)], arrived.at[i]
        )
        for i in range(chunks)
    ]
    for copy in small + large:
        copy.start()
    for copy in small:
        copy.wait()

    def ready(first):
        if first % chunk == 0:
            large[first // chunk].wait()

    src_dst_part(slice_rows, traffic, src[...], dst[...], time[...], time, out, ready)


def time_kernel(traffic, src, dst, time, out):
    src_now, dst_now, time_now = src[...].T, dst[...], time[...]
    rank, src_rows = src_now.shape
    dst_halves = halves(dst_now)
    total = times(gram(src_now) * gram(dst_now), time_now)
    seen_sum = jnp.zeros(total.shape, f32)
    for i in range(src_rows):
        seen = jnp.dot(dst_halves, traffic[i], preferred_element_type=f32)
        seen_sum = seen_sum + (seen[:rank] + seen[rank:]) * src_now[:, i : i + 1]
    out[...] = total - seen_sum


def back(x, offset, position):
    if offset >= x.shape[1]:
        return jnp.zeros_like(x)
    return jnp.where(position >= offset, pltpu.roll(x, offset, 1), 0.0)


def forth(x, offset, position):
    size = x.shape[1]
    if offset >= size:
        return jnp.zeros_like(x)
    return jnp.where(position < size - offset, pltpu.roll(x, size - offset, 1), 0.0)


def smooth_kernel(slice_rows, src_top, blocks, *refs):
    held, time_part, src_time_out, dst_time_out = refs[:blocks], refs[blocks], refs[-2], refs[-1]
    rank, time_rows = time_part.shape
    here = lax.axis_index("tm")
    total = held[0][: src_top + rank]
    for other in held[1:]:
        total = total + other[: src_top + rank]
    src_time_out[:src_top] = total[:src_top]
    src_time_out[src_top:] = time_part[...]
    dst_time_out[:rank] = total[src_top:]
    slices = [h[src_top + rank :] for h in held]
    ordered = []
    for block in range(blocks):
        pick = slices[0]
        for mask in range(1, blocks):
            pick = jnp.where((here ^ block) == mask, slices[mask], pick)
        ordered.append(pick)
    whole = jnp.concatenate(ordered, 1)
    position = lax.broadcasted_iota(jnp.int32, whole.shape, 1)
    hour_diff = jnp.where(position >= 1, whole - back(whole, 1, position), 0.0)
    day_diff = jnp.where(position >= DAY, whole - back(whole, DAY, position), 0.0)
    smooth = hour_weight * (hour_diff - forth(hour_diff, 1, position))
    smooth = smooth + day_weight * (day_diff - forth(day_diff, DAY, position))
    mine = smooth[:, :time_rows]
    for block in range(1, blocks):
        mine = jnp.where(here == block, smooth[:, block * time_rows : (block + 1) * time_rows], mine)
    dst_time_out[rank:] = time_part[...]
    place, smooths = place_of(rank // slice_rows)
    mine = jnp.where(smooths, mine, 0.0)
    start = pl.multiple_of(rank + place * slice_rows, slice_rows)
    dst_time_out[pl.ds(start, slice_rows)] = dst_time_out[pl.ds(start, slice_rows)] + mine


def exchanged(x, src_mask, dst_mask, tm_mask):
    src_size, dst_size, tm_size = (lax.axis_size(a) for a in AXES)
    route = []
    for s in range(src_size):
        for d in range(dst_size):
            for t in range(tm_size):
                here = (s * dst_size + d) * tm_size + t
                there = ((s ^ src_mask) * dst_size + (d ^ dst_mask)) * tm_size + (t ^ tm_mask)
                route.append((here, there))
    return lax.ppermute(x, AXES, route)


def on_device(traffic, src_factor, dst_factor, time_factor):
    src_rows, rank = src_factor.shape
    src_size, dst_size, tm_size = (lax.axis_size(a) for a in AXES)
    slice_rows = max(8, rank // (src_size * dst_size // 2))
    dst_rows, time_rows = dst_factor.shape[0], time_factor.shape[0]
    src_top = rank * src_rows // LANES if src_rows < LANES else src_rows
    mixed_shape = jax.ShapeDtypeStruct((src_top + rank + slice_rows, LANES), f32)
    zero_kernel = pl.pallas_call(
        functools.partial(entry_kernel, slice_rows),
        out_shape=(
            mixed_shape,
            jax.ShapeDtypeStruct(traffic.shape, traffic.dtype),
            jax.ShapeDtypeStruct((src_rows, rank), f32),
            jax.ShapeDtypeStruct((rank, dst_rows), f32),
            jax.ShapeDtypeStruct((rank, time_rows), f32),
        ),
        in_specs=[pl.BlockSpec(memory_space=pltpu.HBM)] * 4,
        out_specs=(VMEM,) * 5,
        scratch_shapes=[pltpu.SemaphoreType.DMA((4 + 3,))],
        compiler_params=PARAMS,
        name="entry",
    )
    first_kernel = pl.pallas_call(
        functools.partial(src_dst_kernel, slice_rows),
        out_shape=mixed_shape,
        in_specs=[VMEM] * 4,
        out_specs=VMEM,
        compiler_params=PARAMS,
        name="src_dst_part",
    )
    second_kernel = pl.pallas_call(
        time_kernel,
        out_shape=jax.ShapeDtypeStruct((rank, time_rows), f32),
        in_specs=[VMEM] * 4,
        out_specs=VMEM,
        compiler_params=PARAMS,
        name="time_part",
    )
    third_kernel = pl.pallas_call(
        functools.partial(smooth_kernel, slice_rows, src_top, tm_size),
        out_shape=(
            jax.ShapeDtypeStruct((src_top + rank, LANES), f32),
            jax.ShapeDtypeStruct((2 * rank, LANES), f32),
        ),
        in_specs=[VMEM] * (tm_size + 1),
        out_specs=(VMEM, VMEM),
        compiler_params=PARAMS,
        name="tm_sums",
    )
    for iteration in range(STEPS):
        if iteration == 0:
            given = (traffic, src_factor, dst_factor.T, time_factor.T)
            given = [pltpu.with_memory_space_constraint(x, pltpu.HBM) for x in given]
            mixed, traffic, src_now, dst_now, time_now = zero_kernel(*given)
        else:
            mixed = first_kernel(traffic, src_now, dst_now, time_now)
        others = [exchanged(mixed, 0, 0, mask) for mask in range(1, tm_size)]
        time_part = second_kernel(traffic, src_now, dst_now, time_now)
        add_time = exchanged(time_part, 2, 1, 0)
        src_time, dst_time = third_kernel(mixed, *others, time_part)
        src_mask, dst_mask = 2, 1
        while src_mask < src_size or dst_mask < dst_size:
            if src_mask > 2:
                src_time = jnp.concatenate([src_sum, dst_time[rank:]], 0)
                both = src_mask < src_size and dst_mask < dst_size
                add_time = exchanged(dst_time[rank:], src_mask, dst_mask, 0) if both else 0.0
            src_sum = src_time[:src_top]
            add_dst = 0.0
            if src_mask < src_size:
                other = exchanged(dst_time, src_mask, 0, 0)
                add_dst, add_time = other[:rank], add_time + other[rank:]
            if dst_mask < dst_size:
                other = exchanged(src_time, 0, dst_mask, 0)
                src_sum, add_time = src_sum + other[:src_top], add_time + other[src_top:]
            dst_time = jnp.concatenate([dst_time[:rank] + add_dst, dst_time[rank:] + add_time], 0)
            src_mask, dst_mask = src_mask * 2, dst_mask * 2
        dst_time = dst_time + exchanged(dst_time, 1, 0, 0)
        grad_src = unpacked(src_sum, rank) / rank
        grad_dst = dst_time[:rank] / rank
        grad_time = dst_time[rank:] / rank
        if iteration + 1 < STEPS:
            src_now = src_now - step_rate * grad_src
            dst_now = dst_now - step_rate * grad_dst
            time_now = time_now - step_rate * grad_time
    return (grad_src, grad_dst.T, grad_time.T)


def solution(mesh):
    in_specs = (P("src", "dst", "tm"), P("src", None), P("dst", None), P("tm", None))
    out_specs = (P("src", None), P("dst", None), P("tm", None))
    return jax.shard_map(
        on_device, mesh=mesh, in_specs=in_specs, out_specs=out_specs, check_vma=False
    )
```

```python
import functools

import jax
import jax.numpy as jnp
from jax import lax
from jax.experimental import pallas as pl
from jax.experimental.pallas import tpu as pltpu
from jax.sharding import PartitionSpec as P


DAY = 288
STEPS = 3

hour_weight = 32.0
day_weight = 64.0
step_rate = 0.1
highest = lax.Precision.HIGHEST
f32 = jnp.float32
bf16 = jnp.bfloat16
LANES = 128
AXES = ("src", "dst", "tm")
BY_LANES = (((1,), (1,)), ((), ()))
VMEM = pl.BlockSpec(memory_space=pltpu.VMEM)
PARAMS = pltpu.CompilerParams(vmem_limit_bytes=24 << 20)


def halves(x):
    high = x.astype(bf16)
    low = (x - high.astype(f32)).astype(bf16)
    return jnp.concatenate([high, low], 0)


def gram(x):
    return lax.dot_general(x, x, BY_LANES, precision=highest, preferred_element_type=f32)


def times(a, b):
    return jnp.dot(a, b, precision=highest, preferred_element_type=f32)


def packed(x):
    fold = LANES // x.shape[1] if x.shape[1] < LANES else 1
    rows = x.shape[0] // fold
    return x if fold == 1 else jnp.concatenate([x[i * rows : (i + 1) * rows] for i in range(fold)], 1)


def unpacked(x, columns):
    fold = x.shape[1] // columns
    return x if fold == 1 else jnp.concatenate([x[:, i * columns : (i + 1) * columns] for i in range(fold)], 0)


def place_of(count, core=0):
    place = (lax.axis_index("src") ^ core) * (lax.axis_size("dst") // 2) + lax.axis_index("dst") // 2
    return jnp.minimum(place, count - 1), place < count


def src_dst_part(slice_rows, traffic, src_now, dst_now, time_now, time, out, ready=None):
    rank = src_now.shape[1]
    src_rows, dst_rows, time_rows = traffic.shape
    time_gram = gram(time_now)
    src_model = times(src_now, gram(dst_now) * time_gram)
    dst_model = times(gram(src_now.T) * time_gram, dst_now)
    time_halves = halves(time_now)
    dst_wide = jnp.concatenate([dst_now, dst_now], 0).T
    src_wide = jnp.concatenate([src_now, src_now], 1)
    dst_sum = jnp.zeros((dst_rows, 2 * rank), f32)
    rows = []
    step = 4
    for first in range(0, src_rows, step):
        if ready is not None:
            ready(first)
        block = traffic[first : first + step].reshape(step * dst_rows, time_rows)
        seen = lax.dot_general(block, time_halves, BY_LANES, preferred_element_type=f32)
        for i in range(step):
            part = seen[i * dst_rows : (i + 1) * dst_rows]
            dst_sum = dst_sum + part * src_wide[first + i : first + i + 1]
            rows.append(jnp.sum(part * dst_wide, axis=0, keepdims=True))
    src_sum = jnp.concatenate(rows, 0)
    dst_seen = (dst_sum[:, :rank] + dst_sum[:, rank:]).T
    src_part = src_model - (src_sum[:, :rank] + src_sum[:, rank:])
    dst_part = dst_model - dst_seen
    src_packed = packed(src_part)
    top = src_packed.shape[0]
    out[:top] = src_packed
    out[top : top + rank] = dst_part
    start = pl.multiple_of(place_of(rank // slice_rows)[0] * slice_rows, slice_rows)
    out[top + rank :] = time[pl.ds(start, slice_rows)]


def src_dst_kernel(slice_rows, traffic, src, dst, time, out):
    src_dst_part(slice_rows, traffic, src[...], dst[...], time[...], time, out)


def entry_kernel(slice_rows, traffic_in, src_in, dst_in, time_in, out, traffic, src, dst, time, arrived):
    chunks = arrived.shape[0] - 3
    chunk = traffic.shape[0] // chunks
    small = [
        pltpu.make_async_copy(a, b, arrived.at[chunks + i])
        for i, (a, b) in enumerate(((src_in, src), (dst_in, dst), (time_in, time)))
    ]
    large = [
        pltpu.make_async_copy(
            traffic_in.at[pl.ds(i * chunk, chunk)], traffic.at[pl.ds(i * chunk, chunk)], arrived.at[i]
        )
        for i in range(chunks)
    ]
    for copy in small + large:
        copy.start()
    for copy in small:
        copy.wait()

    def ready(first):
        if first % chunk == 0:
            large[first // chunk].wait()

    src_dst_part(slice_rows, traffic, src[...], dst[...], time[...], time, out, ready)


def time_kernel(traffic, src, dst, time, out):
    src_now, dst_now, time_now = src[...].T, dst[...], time[...]
    rank, src_rows = src_now.shape
    dst_halves = halves(dst_now)
    total = times(gram(src_now) * gram(dst_now), time_now)
    seen_sum = jnp.zeros(total.shape, f32)
    for i in range(src_rows):
        seen = jnp.dot(dst_halves, traffic[i], preferred_element_type=f32)
        seen_sum = seen_sum + (seen[:rank] + seen[rank:]) * src_now[:, i : i + 1]
    out[...] = total - seen_sum


def back(x, offset, position):
    if offset >= x.shape[1]:
        return jnp.zeros_like(x)
    return jnp.where(position >= offset, pltpu.roll(x, offset, 1), 0.0)


def forth(x, offset, position):
    size = x.shape[1]
    if offset >= size:
        return jnp.zeros_like(x)
    return jnp.where(position < size - offset, pltpu.roll(x, size - offset, 1), 0.0)


def smooth_kernel(slice_rows, src_top, blocks, *refs):
    held, time_part, src_time_out, dst_out = refs[:blocks], refs[blocks], *refs[-2:]
    rank, time_rows = time_part.shape
    here = lax.axis_index("tm")
    total = held[0][: src_top + rank]
    for other in held[1:]:
        total = total + other[: src_top + rank]
    src_time_out[:src_top] = total[:src_top]
    src_time_out[src_top:] = time_part[...]
    dst_out[:rank] = total[src_top:]
    slices = [h[src_top + rank :] for h in held]
    ordered = []
    for block in range(blocks):
        pick = slices[0]
        for mask in range(1, blocks):
            pick = jnp.where((here ^ block) == mask, slices[mask], pick)
        ordered.append(pick)
    whole = jnp.concatenate(ordered, 1)
    position = lax.broadcasted_iota(jnp.int32, whole.shape, 1)
    hour_diff = jnp.where(position >= 1, whole - back(whole, 1, position), 0.0)
    day_diff = jnp.where(position >= DAY, whole - back(whole, DAY, position), 0.0)
    smooth = hour_weight * (hour_diff - forth(hour_diff, 1, position))
    smooth = smooth + day_weight * (day_diff - forth(day_diff, DAY, position))
    mine = smooth[:, :time_rows]
    for block in range(1, blocks):
        mine = jnp.where(here == block, smooth[:, block * time_rows : (block + 1) * time_rows], mine)
    dst_out[rank:] = jnp.where(place_of(rank // slice_rows)[1], mine, 0.0)


def join_kernel(slice_rows, own, other, time_part, out):
    rank = time_part.shape[0]
    out[:rank] = own[:rank] + other[:rank]
    out[rank:] = time_part[...]
    for core, given in enumerate((own, other)):
        place = place_of(rank // slice_rows, core)[0]
        rows = pl.ds(pl.multiple_of(rank + place * slice_rows, slice_rows), slice_rows)
        out[rows] = out[rows] + given[rank:]


def exchanged(x, src_mask, dst_mask, tm_mask):
    src_size, dst_size, tm_size = (lax.axis_size(a) for a in AXES)
    route = []
    for s in range(src_size):
        for d in range(dst_size):
            for t in range(tm_size):
                here = (s * dst_size + d) * tm_size + t
                there = ((s ^ src_mask) * dst_size + (d ^ dst_mask)) * tm_size + (t ^ tm_mask)
                route.append((here, there))
    return lax.ppermute(x, AXES, route)


def on_device(traffic, src_factor, dst_factor, time_factor):
    src_rows, rank = src_factor.shape
    src_size, dst_size, tm_size = (lax.axis_size(a) for a in AXES)
    slice_rows = max(8, rank // (src_size * dst_size // 2))
    dst_rows, time_rows = dst_factor.shape[0], time_factor.shape[0]
    src_top = rank * src_rows // LANES if src_rows < LANES else src_rows
    mixed_shape = jax.ShapeDtypeStruct((src_top + rank + slice_rows, LANES), f32)
    zero_kernel = pl.pallas_call(
        functools.partial(entry_kernel, slice_rows),
        out_shape=(
            mixed_shape,
            jax.ShapeDtypeStruct(traffic.shape, traffic.dtype),
            jax.ShapeDtypeStruct((src_rows, rank), f32),
            jax.ShapeDtypeStruct((rank, dst_rows), f32),
            jax.ShapeDtypeStruct((rank, time_rows), f32),
        ),
        in_specs=[pl.BlockSpec(memory_space=pltpu.HBM)] * 4,
        out_specs=(VMEM,) * 5,
        scratch_shapes=[pltpu.SemaphoreType.DMA((4 + 3,))],
        compiler_params=PARAMS,
        name="entry",
    )
    first_kernel = pl.pallas_call(
        functools.partial(src_dst_kernel, slice_rows),
        out_shape=mixed_shape,
        in_specs=[VMEM] * 4,
        out_specs=VMEM,
        compiler_params=PARAMS,
        name="src_dst_part",
    )
    second_kernel = pl.pallas_call(
        time_kernel,
        out_shape=jax.ShapeDtypeStruct((rank, time_rows), f32),
        in_specs=[VMEM] * 4,
        out_specs=VMEM,
        compiler_params=PARAMS,
        name="time_part",
    )
    third_kernel = pl.pallas_call(
        functools.partial(smooth_kernel, slice_rows, src_top, tm_size),
        out_shape=(
            jax.ShapeDtypeStruct((src_top + rank, LANES), f32),
            jax.ShapeDtypeStruct((rank + slice_rows, dst_rows), f32),
        ),
        in_specs=[VMEM] * (tm_size + 1),
        out_specs=(VMEM,) * 2,
        compiler_params=PARAMS,
        name="tm_sums",
    )
    join = pl.pallas_call(
        functools.partial(join_kernel, slice_rows),
        out_shape=jax.ShapeDtypeStruct((2 * rank, LANES), f32),
        in_specs=[VMEM] * 3,
        out_specs=VMEM,
        compiler_params=PARAMS,
        name="join",
    )
    for iteration in range(STEPS):
        if iteration == 0:
            given = (traffic, src_factor, dst_factor.T, time_factor.T)
            given = [pltpu.with_memory_space_constraint(x, pltpu.HBM) for x in given]
            mixed, traffic, src_now, dst_now, time_now = zero_kernel(*given)
        else:
            mixed = first_kernel(traffic, src_now, dst_now, time_now)
        others = []
        for mask in range(1, tm_size):
            others.append(exchanged(mixed, 0, 0, mask))
        time_part = second_kernel(traffic, src_now, dst_now, time_now)
        time_part = time_part + exchanged(time_part, 1, 0, 0)
        add_time = exchanged(time_part, 2, 1, 0)
        src_time, dst_smooth = third_kernel(mixed, *others, time_part)
        other_smooth = exchanged(dst_smooth, 1, 0, 0)
        dst_time = join(dst_smooth, other_smooth, time_part)
        src_mask, dst_mask = 2, 1
        while src_mask < src_size or dst_mask < dst_size:
            if src_mask > 2:
                src_time = jnp.concatenate([src_sum, dst_time[rank:]], 0)
                both = src_mask < src_size and dst_mask < dst_size
                add_time = exchanged(dst_time[rank:], src_mask, dst_mask, 0) if both else 0.0
            src_sum = src_time[:src_top]
            add_dst = 0.0
            if dst_mask < dst_size:
                other = exchanged(src_time, 0, dst_mask, 0)
                src_sum, add_time = src_sum + other[:src_top], add_time + other[src_top:]
            if src_mask < src_size:
                other = exchanged(dst_time, src_mask, 0, 0)
                add_dst, add_time = other[:rank], add_time + other[rank:]
            dst_time = jnp.concatenate([dst_time[:rank] + add_dst, dst_time[rank:] + add_time], 0)
            src_mask, dst_mask = src_mask * 2, dst_mask * 2
        grad_src = unpacked(src_sum, rank) / rank
        grad_dst = dst_time[:rank] / rank
        grad_time = dst_time[rank:] / rank
        if iteration + 1 < STEPS:
            src_now = src_now - step_rate * grad_src
            dst_now = dst_now - step_rate * grad_dst
            time_now = time_now - step_rate * grad_time
    return (grad_src, grad_dst.T, grad_time.T)


def solution(mesh):
    in_specs = (P("src", "dst", "tm"), P("src", None), P("dst", None), P("tm", None))
    out_specs = (P("src", None), P("dst", None), P("tm", None))
    return jax.shard_map(
        on_device, mesh=mesh, in_specs=in_specs, out_specs=out_specs, check_vma=False
    )
```

```python
import functools

import jax
import jax.numpy as jnp
from jax import lax
from jax.experimental import pallas as pl
from jax.experimental.pallas import tpu as pltpu
from jax.sharding import PartitionSpec as P


DAY = 288
STEPS = 3

hour_weight = 32.0
day_weight = 64.0
step_rate = 0.1
f32 = jnp.float32
bf16 = jnp.bfloat16
LANES = 128
AXES = ("src", "dst", "tm")
BY_LANES = (((1,), (1,)), ((), ()))
VMEM = pl.BlockSpec(memory_space=pltpu.VMEM)
PARAMS = pltpu.CompilerParams(vmem_limit_bytes=24 << 20)


def split(x):
    high = x.astype(bf16)
    return high, (x - high.astype(f32)).astype(bf16)


def halves(x):
    return jnp.concatenate(split(x), 0)


def gram(x):
    high, low = split(x)
    left, right = jnp.concatenate([high, high, low], 1), jnp.concatenate([high, low, high], 1)
    return lax.dot_general(left, right, BY_LANES, preferred_element_type=f32)


def times(a, b):
    (a_high, a_low), (b_high, b_low) = split(a), split(b)
    product = jnp.dot(a_high, b_high, preferred_element_type=f32)
    product = product + jnp.dot(a_high, b_low, preferred_element_type=f32)
    return product + jnp.dot(a_low, b_high, preferred_element_type=f32)


def packed(x):
    fold = LANES // x.shape[1] if x.shape[1] < LANES else 1
    rows = x.shape[0] // fold
    return x if fold == 1 else jnp.concatenate([x[i * rows : (i + 1) * rows] for i in range(fold)], 1)


def unpacked(x, columns):
    fold = x.shape[1] // columns
    return x if fold == 1 else jnp.concatenate([x[:, i * columns : (i + 1) * columns] for i in range(fold)], 0)


def place_of(count, core=0):
    place = (lax.axis_index("src") ^ core) * (lax.axis_size("dst") // 2) + lax.axis_index("dst") // 2
    return jnp.minimum(place, count - 1), place < count


def src_dst_part(slice_rows, traffic, src_now, dst_now, time_now, time, out, ready=None):
    rank = src_now.shape[1]
    src_rows, dst_rows, time_rows = traffic.shape
    time_gram = gram(time_now)
    src_model = times(src_now, gram(dst_now) * time_gram)
    dst_model = times(gram(src_now.T) * time_gram, dst_now)
    time_halves = halves(time_now)
    dst_wide = jnp.concatenate([dst_now, dst_now], 0).T
    src_wide = jnp.concatenate([src_now, src_now], 1)
    dst_sum = jnp.zeros((dst_rows, 2 * rank), f32)
    rows = []
    step = 4
    for first in range(0, src_rows, step):
        if ready is not None:
            ready(first)
        block = traffic[first : first + step].reshape(step * dst_rows, time_rows)
        seen = lax.dot_general(block, time_halves, BY_LANES, preferred_element_type=f32)
        for i in range(step):
            part = seen[i * dst_rows : (i + 1) * dst_rows]
            dst_sum = dst_sum + part * src_wide[first + i : first + i + 1]
            rows.append(jnp.sum(part * dst_wide, axis=0, keepdims=True))
    src_sum = jnp.concatenate(rows, 0)
    dst_seen = (dst_sum[:, :rank] + dst_sum[:, rank:]).T
    src_part = src_model - (src_sum[:, :rank] + src_sum[:, rank:])
    dst_part = dst_model - dst_seen
    src_packed = packed(src_part)
    top = src_packed.shape[0]
    out[:top] = src_packed
    out[top : top + rank] = dst_part
    start = pl.multiple_of(place_of(rank // slice_rows)[0] * slice_rows, slice_rows)
    out[top + rank :] = time[pl.ds(start, slice_rows)]


def src_dst_kernel(slice_rows, traffic, src, dst, time, out):
    src_dst_part(slice_rows, traffic, src[...], dst[...], time[...], time, out)


def entry_kernel(slice_rows, traffic_in, src_in, dst_in, time_in, out, traffic, src, dst, time, arrived):
    chunks = arrived.shape[0] - 3
    chunk = traffic.shape[0] // chunks
    small = [
        pltpu.make_async_copy(a, b, arrived.at[chunks + i])
        for i, (a, b) in enumerate(((src_in, src), (dst_in, dst), (time_in, time)))
    ]
    large = [
        pltpu.make_async_copy(
            traffic_in.at[pl.ds(i * chunk, chunk)], traffic.at[pl.ds(i * chunk, chunk)], arrived.at[i]
        )
        for i in range(chunks)
    ]
    for copy in small + large:
        copy.start()
    for copy in small:
        copy.wait()

    def ready(first):
        if first % chunk == 0:
            large[first // chunk].wait()

    src_dst_part(slice_rows, traffic, src[...], dst[...], time[...], time, out, ready)


def time_kernel(traffic, src, dst, time, out):
    src_now, dst_now, time_now = src[...].T, dst[...], time[...]
    rank, src_rows = src_now.shape
    dst_halves = halves(dst_now)
    total = times(gram(src_now) * gram(dst_now), time_now)
    seen_sum = jnp.zeros(total.shape, f32)
    for i in range(src_rows):
        seen = jnp.dot(dst_halves, traffic[i], preferred_element_type=f32)
        seen_sum = seen_sum + (seen[:rank] + seen[rank:]) * src_now[:, i : i + 1]
    out[...] = total - seen_sum


def back(x, offset, position):
    if offset >= x.shape[1]:
        return jnp.zeros_like(x)
    return jnp.where(position >= offset, pltpu.roll(x, offset, 1), 0.0)


def forth(x, offset, position):
    size = x.shape[1]
    if offset >= size:
        return jnp.zeros_like(x)
    return jnp.where(position < size - offset, pltpu.roll(x, size - offset, 1), 0.0)


def smooth_kernel(slice_rows, src_top, blocks, *refs):
    held, time_part, src_time_out, dst_out = refs[:blocks], refs[blocks], *refs[-2:]
    rank, time_rows = time_part.shape
    here = lax.axis_index("tm")
    total = held[0][: src_top + rank]
    for other in held[1:]:
        total = total + other[: src_top + rank]
    src_time_out[:src_top] = total[:src_top]
    src_time_out[src_top:] = time_part[...]
    dst_out[:rank] = total[src_top:]
    slices = [h[src_top + rank :] for h in held]
    ordered = []
    for block in range(blocks):
        pick = slices[0]
        for mask in range(1, blocks):
            pick = jnp.where((here ^ block) == mask, slices[mask], pick)
        ordered.append(pick)
    whole = jnp.concatenate(ordered, 1)
    position = lax.broadcasted_iota(jnp.int32, whole.shape, 1)
    hour_diff = jnp.where(position >= 1, whole - back(whole, 1, position), 0.0)
    day_diff = jnp.where(position >= DAY, whole - back(whole, DAY, position), 0.0)
    smooth = hour_weight * (hour_diff - forth(hour_diff, 1, position))
    smooth = smooth + day_weight * (day_diff - forth(day_diff, DAY, position))
    mine = smooth[:, :time_rows]
    for block in range(1, blocks):
        mine = jnp.where(here == block, smooth[:, block * time_rows : (block + 1) * time_rows], mine)
    dst_out[rank:] = jnp.where(place_of(rank // slice_rows)[1], mine, 0.0)


def join_kernel(slice_rows, own, other, time_part, out):
    rank = time_part.shape[0]
    out[:rank] = own[:rank] + other[:rank]
    out[rank:] = time_part[...]
    for core, given in enumerate((own, other)):
        place = place_of(rank // slice_rows, core)[0]
        rows = pl.ds(pl.multiple_of(rank + place * slice_rows, slice_rows), slice_rows)
        out[rows] = out[rows] + given[rank:]


def exchanged(x, src_mask, dst_mask, tm_mask):
    src_size, dst_size, tm_size = (lax.axis_size(a) for a in AXES)
    route = []
    for s in range(src_size):
        for d in range(dst_size):
            for t in range(tm_size):
                here = (s * dst_size + d) * tm_size + t
                there = ((s ^ src_mask) * dst_size + (d ^ dst_mask)) * tm_size + (t ^ tm_mask)
                route.append((here, there))
    return lax.ppermute(x, AXES, route)


def on_device(traffic, src_factor, dst_factor, time_factor):
    src_rows, rank = src_factor.shape
    src_size, dst_size, tm_size = (lax.axis_size(a) for a in AXES)
    slice_rows = max(8, rank // (src_size * dst_size // 2))
    dst_rows, time_rows = dst_factor.shape[0], time_factor.shape[0]
    src_top = rank * src_rows // LANES if src_rows < LANES else src_rows
    mixed_shape = jax.ShapeDtypeStruct((src_top + rank + slice_rows, LANES), f32)
    zero_kernel = pl.pallas_call(
        functools.partial(entry_kernel, slice_rows),
        out_shape=(
            mixed_shape,
            jax.ShapeDtypeStruct(traffic.shape, traffic.dtype),
            jax.ShapeDtypeStruct((src_rows, rank), f32),
            jax.ShapeDtypeStruct((rank, dst_rows), f32),
            jax.ShapeDtypeStruct((rank, time_rows), f32),
        ),
        in_specs=[pl.BlockSpec(memory_space=pltpu.HBM)] * 4,
        out_specs=(VMEM,) * 5,
        scratch_shapes=[pltpu.SemaphoreType.DMA((4 + 3,))],
        compiler_params=PARAMS,
        name="entry",
    )
    first_kernel = pl.pallas_call(
        functools.partial(src_dst_kernel, slice_rows),
        out_shape=mixed_shape,
        in_specs=[VMEM] * 4,
        out_specs=VMEM,
        compiler_params=PARAMS,
        name="src_dst_part",
    )
    second_kernel = pl.pallas_call(
        time_kernel,
        out_shape=jax.ShapeDtypeStruct((rank, time_rows), f32),
        in_specs=[VMEM] * 4,
        out_specs=VMEM,
        compiler_params=PARAMS,
        name="time_part",
    )
    third_kernel = pl.pallas_call(
        functools.partial(smooth_kernel, slice_rows, src_top, tm_size),
        out_shape=(
            jax.ShapeDtypeStruct((src_top + rank, LANES), f32),
            jax.ShapeDtypeStruct((rank + slice_rows, dst_rows), f32),
        ),
        in_specs=[VMEM] * (tm_size + 1),
        out_specs=(VMEM,) * 2,
        compiler_params=PARAMS,
        name="tm_sums",
    )
    join = pl.pallas_call(
        functools.partial(join_kernel, slice_rows),
        out_shape=jax.ShapeDtypeStruct((2 * rank, LANES), f32),
        in_specs=[VMEM] * 3,
        out_specs=VMEM,
        compiler_params=PARAMS,
        name="join",
    )
    for iteration in range(STEPS):
        if iteration == 0:
            given = (traffic, src_factor, dst_factor.T, time_factor.T)
            given = [pltpu.with_memory_space_constraint(x, pltpu.HBM) for x in given]
            mixed, traffic, src_now, dst_now, time_now = zero_kernel(*given)
        else:
            mixed = first_kernel(traffic, src_now, dst_now, time_now)
        others = []
        for mask in range(1, tm_size):
            others.append(exchanged(mixed, 0, 0, mask))
        time_part = second_kernel(traffic, src_now, dst_now, time_now)
        add_time = exchanged(time_part, 2, 1, 0)
        time_part = time_part + exchanged(time_part, 1, 0, 0)
        add_time = add_time + exchanged(add_time, 1, 0, 0)
        src_time, dst_smooth = third_kernel(mixed, *others, time_part)
        other_smooth = exchanged(dst_smooth, 1, 0, 0)
        dst_time = join(dst_smooth, other_smooth, time_part)
        src_mask, dst_mask = 2, 1
        while src_mask < src_size or dst_mask < dst_size:
            if src_mask > 2:
                src_time = jnp.concatenate([src_sum, dst_time[rank:]], 0)
                both = src_mask < src_size and dst_mask < dst_size
                add_time = exchanged(dst_time[rank:], src_mask, dst_mask, 0) if both else 0.0
            src_sum = src_time[:src_top]
            add_dst = 0.0
            if dst_mask < dst_size:
                other = exchanged(src_time, 0, dst_mask, 0)
                src_sum, add_time = src_sum + other[:src_top], add_time + other[src_top:]
            if src_mask < src_size:
                other = exchanged(dst_time, src_mask, 0, 0)
                add_dst, add_time = other[:rank], add_time + other[rank:]
            dst_time = jnp.concatenate([dst_time[:rank] + add_dst, dst_time[rank:] + add_time], 0)
            src_mask, dst_mask = src_mask * 2, dst_mask * 2
        grad_src = unpacked(src_sum, rank) / rank
        grad_dst = dst_time[:rank] / rank
        grad_time = dst_time[rank:] / rank
        if iteration + 1 < STEPS:
            src_now = src_now - step_rate * grad_src
            dst_now = dst_now - step_rate * grad_dst
            time_now = time_now - step_rate * grad_time
    return (grad_src, grad_dst.T, grad_time.T)


def solution(mesh):
    in_specs = (P("src", "dst", "tm"), P("src", None), P("dst", None), P("tm", None))
    out_specs = (P("src", None), P("dst", None), P("tm", None))
    return jax.shard_map(
        on_device, mesh=mesh, in_specs=in_specs, out_specs=out_specs, check_vma=False
    )
```

```python
import functools

import jax
import jax.numpy as jnp
from jax import lax
from jax.experimental import pallas as pl
from jax.experimental.pallas import tpu as pltpu
from jax.sharding import PartitionSpec as P


DAY = 288
STEPS = 3

hour_weight = 32.0
day_weight = 64.0
step_rate = 0.1
f32 = jnp.float32
bf16 = jnp.bfloat16
LANES = 128
AXES = ("src", "dst", "tm")
BY_LANES = (((1,), (1,)), ((), ()))
VMEM = pl.BlockSpec(memory_space=pltpu.VMEM)
PARAMS = pltpu.CompilerParams(vmem_limit_bytes=24 << 20)


def split(x):
    high = x.astype(bf16)
    return high, (x - high.astype(f32)).astype(bf16)


def halves(x):
    return jnp.concatenate(split(x), 0)


def gram(x):
    high = x.astype(bf16)
    rest = x - high.astype(f32)
    middle = rest.astype(bf16)
    low = (rest - middle.astype(f32)).astype(bf16)
    left = jnp.concatenate([high, high, middle, middle, high, low], 1)
    right = jnp.concatenate([high, middle, high, middle, low, high], 1)
    return lax.dot_general(left, right, BY_LANES, preferred_element_type=f32)


def times(a, b):
    return jnp.dot(a, b, precision=lax.Precision.HIGHEST, preferred_element_type=f32)


def packed(x):
    fold = LANES // x.shape[1] if x.shape[1] < LANES else 1
    rows = x.shape[0] // fold
    return x if fold == 1 else jnp.concatenate([x[i * rows : (i + 1) * rows] for i in range(fold)], 1)


def unpacked(x, columns):
    fold = x.shape[1] // columns
    return x if fold == 1 else jnp.concatenate([x[:, i * columns : (i + 1) * columns] for i in range(fold)], 0)


def place_of(count, core=0):
    place = (lax.axis_index("src") ^ core) * (lax.axis_size("dst") // 2) + lax.axis_index("dst") // 2
    return jnp.minimum(place, count - 1), place < count


def src_dst_part(slice_rows, traffic, src_now, dst_now, time_now, time, out, partial, ready=None):
    rank = src_now.shape[1]
    src_rows, dst_rows, time_rows = traffic.shape
    time_gram = gram(time_now)
    src_model = times(src_now, gram(dst_now) * time_gram)
    dst_model = times(gram(src_now.T) * time_gram, dst_now)
    time_halves = halves(time_now)
    dst_wide = jnp.concatenate([dst_now, dst_now], 0).T
    src_wide = jnp.concatenate([src_now, src_now], 1)
    dst_sum = jnp.zeros((dst_rows, 2 * rank), f32)
    step = 8
    for first in range(0, src_rows, step):
        if ready is not None:
            ready(first)
        block = traffic[first : first + step].reshape(step * dst_rows, time_rows)
        seen = lax.dot_general(block, time_halves, BY_LANES, preferred_element_type=f32)
        for i in range(step):
            part = seen[i * dst_rows : (i + 1) * dst_rows]
            dst_sum = dst_sum + part * src_wide[first + i : first + i + 1]
            eights = (part * dst_wide).reshape(dst_rows // 8, 8, 2 * rank)
            partial[(first + i) * 8 : (first + i + 1) * 8] = jnp.sum(eights, axis=0)
    src_sum = partial[pl.ds(0, src_rows, stride=8)]
    for i in range(1, 8):
        src_sum = src_sum + partial[pl.ds(i, src_rows, stride=8)]
    dst_seen = (dst_sum[:, :rank] + dst_sum[:, rank:]).T
    src_part = src_model - (src_sum[:, :rank] + src_sum[:, rank:])
    dst_part = dst_model - dst_seen
    src_packed = packed(src_part)
    top = src_packed.shape[0]
    out[:top] = src_packed
    out[top : top + rank] = dst_part
    start = pl.multiple_of(place_of(rank // slice_rows)[0] * slice_rows, slice_rows)
    out[top + rank :] = time[pl.ds(start, slice_rows)]


def src_dst_kernel(slice_rows, traffic, src, dst, time, out, partial):
    src_dst_part(slice_rows, traffic, src[...], dst[...], time[...], time, out, partial)


def entry_kernel(slice_rows, traffic_in, src_in, dst_in, time_in, out, traffic, src, dst, time, partial, arrived):
    chunks = arrived.shape[0] - 3
    chunk = traffic.shape[0] // chunks
    small = [
        pltpu.make_async_copy(a, b, arrived.at[chunks + i])
        for i, (a, b) in enumerate(((src_in, src), (dst_in, dst), (time_in, time)))
    ]
    large = [
        pltpu.make_async_copy(
            traffic_in.at[pl.ds(i * chunk, chunk)], traffic.at[pl.ds(i * chunk, chunk)], arrived.at[i]
        )
        for i in range(chunks)
    ]
    for copy in small + large:
        copy.start()
    for copy in small:
        copy.wait()

    def ready(first):
        if first % chunk == 0:
            large[first // chunk].wait()

    src_dst_part(slice_rows, traffic, src[...], dst[...], time[...], time, out, partial, ready)


def time_kernel(traffic, src, dst, time, out):
    src_now, dst_now, time_now = src[...].T, dst[...], time[...]
    rank, src_rows = src_now.shape
    dst_halves = halves(dst_now)
    total = times(gram(src_now) * gram(dst_now), time_now)
    seen_sum = jnp.zeros(total.shape, f32)
    for i in range(src_rows):
        seen = jnp.dot(dst_halves, traffic[i], preferred_element_type=f32)
        seen_sum = seen_sum + (seen[:rank] + seen[rank:]) * src_now[:, i : i + 1]
    out[...] = total - seen_sum


def back(x, offset, position):
    if offset >= x.shape[1]:
        return jnp.zeros_like(x)
    return jnp.where(position >= offset, pltpu.roll(x, offset, 1), 0.0)


def forth(x, offset, position):
    size = x.shape[1]
    if offset >= size:
        return jnp.zeros_like(x)
    return jnp.where(position < size - offset, pltpu.roll(x, size - offset, 1), 0.0)


def smooth_kernel(slice_rows, src_top, blocks, *refs):
    held, time_part, src_time_out, dst_out = refs[:blocks], refs[blocks], *refs[-2:]
    rank, time_rows = time_part.shape
    here = lax.axis_index("tm")
    total = held[0][: src_top + rank]
    for other in held[1:]:
        total = total + other[: src_top + rank]
    src_time_out[:src_top] = total[:src_top]
    src_time_out[src_top:] = time_part[...]
    dst_out[:rank] = total[src_top:]
    slices = [h[src_top + rank :] for h in held]
    ordered = []
    for block in range(blocks):
        pick = slices[0]
        for mask in range(1, blocks):
            pick = jnp.where((here ^ block) == mask, slices[mask], pick)
        ordered.append(pick)
    whole = jnp.concatenate(ordered, 1)
    position = lax.broadcasted_iota(jnp.int32, whole.shape, 1)
    hour_diff = jnp.where(position >= 1, whole - back(whole, 1, position), 0.0)
    day_diff = jnp.where(position >= DAY, whole - back(whole, DAY, position), 0.0)
    smooth = hour_weight * (hour_diff - forth(hour_diff, 1, position))
    smooth = smooth + day_weight * (day_diff - forth(day_diff, DAY, position))
    mine = smooth[:, :time_rows]
    for block in range(1, blocks):
        mine = jnp.where(here == block, smooth[:, block * time_rows : (block + 1) * time_rows], mine)
    dst_out[rank:] = jnp.where(place_of(rank // slice_rows)[1], mine, 0.0)


def join_kernel(slice_rows, own, other, time_part, out):
    rank = time_part.shape[0]
    out[:rank] = own[:rank] + other[:rank]
    out[rank:] = time_part[...]
    for core, given in enumerate((own, other)):
        place = place_of(rank // slice_rows, core)[0]
        rows = pl.ds(pl.multiple_of(rank + place * slice_rows, slice_rows), slice_rows)
        out[rows] = out[rows] + given[rank:]


def exchanged(x, src_mask, dst_mask, tm_mask):
    src_size, dst_size, tm_size = (lax.axis_size(a) for a in AXES)
    route = []
    for s in range(src_size):
        for d in range(dst_size):
            for t in range(tm_size):
                here = (s * dst_size + d) * tm_size + t
                there = ((s ^ src_mask) * dst_size + (d ^ dst_mask)) * tm_size + (t ^ tm_mask)
                route.append((here, there))
    return lax.ppermute(x, AXES, route)


def on_device(traffic, src_factor, dst_factor, time_factor):
    src_rows, rank = src_factor.shape
    src_size, dst_size, tm_size = (lax.axis_size(a) for a in AXES)
    slice_rows = max(8, rank // (src_size * dst_size // 2))
    dst_rows, time_rows = dst_factor.shape[0], time_factor.shape[0]
    src_top = rank * src_rows // LANES if src_rows < LANES else src_rows
    mixed_shape = jax.ShapeDtypeStruct((src_top + rank + slice_rows, LANES), f32)
    partial_sums = pltpu.VMEM((src_rows * 8 + 8, 2 * rank), f32)
    zero_kernel = pl.pallas_call(
        functools.partial(entry_kernel, slice_rows),
        out_shape=(
            mixed_shape,
            jax.ShapeDtypeStruct(traffic.shape, traffic.dtype),
            jax.ShapeDtypeStruct((src_rows, rank), f32),
            jax.ShapeDtypeStruct((rank, dst_rows), f32),
            jax.ShapeDtypeStruct((rank, time_rows), f32),
        ),
        in_specs=[pl.BlockSpec(memory_space=pltpu.HBM)] * 4,
        out_specs=(VMEM,) * 5,
        scratch_shapes=[partial_sums, pltpu.SemaphoreType.DMA((2 + 3,))],
        compiler_params=PARAMS,
        name="entry",
    )
    first_kernel = pl.pallas_call(
        functools.partial(src_dst_kernel, slice_rows),
        out_shape=mixed_shape,
        in_specs=[VMEM] * 4,
        out_specs=VMEM,
        scratch_shapes=[partial_sums],
        compiler_params=PARAMS,
        name="src_dst_part",
    )
    second_kernel = pl.pallas_call(
        time_kernel,
        out_shape=jax.ShapeDtypeStruct((rank, time_rows), f32),
        in_specs=[VMEM] * 4,
        out_specs=VMEM,
        compiler_params=PARAMS,
        name="time_part",
    )
    third_kernel = pl.pallas_call(
        functools.partial(smooth_kernel, slice_rows, src_top, tm_size),
        out_shape=(
            jax.ShapeDtypeStruct((src_top + rank, LANES), f32),
            jax.ShapeDtypeStruct((rank + slice_rows, dst_rows), f32),
        ),
        in_specs=[VMEM] * (tm_size + 1),
        out_specs=(VMEM,) * 2,
        compiler_params=PARAMS,
        name="tm_sums",
    )
    join = pl.pallas_call(
        functools.partial(join_kernel, slice_rows),
        out_shape=jax.ShapeDtypeStruct((2 * rank, LANES), f32),
        in_specs=[VMEM] * 3,
        out_specs=VMEM,
        compiler_params=PARAMS,
        name="join",
    )
    for iteration in range(STEPS):
        if iteration == 0:
            given = (traffic, src_factor, dst_factor.T, time_factor.T)
            given = [pltpu.with_memory_space_constraint(x, pltpu.HBM) for x in given]
            mixed, traffic, src_now, dst_now, time_now = zero_kernel(*given)
        else:
            mixed = first_kernel(traffic, src_now, dst_now, time_now)
        others = []
        for mask in range(1, tm_size):
            others.append(exchanged(mixed, 0, 0, mask))
        time_part = second_kernel(traffic, src_now, dst_now, time_now)
        add_time = exchanged(time_part, 2, 1, 0)
        time_part = time_part + exchanged(time_part, 1, 0, 0)
        add_time = add_time + exchanged(add_time, 1, 0, 0)
        src_time, dst_smooth = third_kernel(mixed, *others, time_part)
        other_smooth = exchanged(dst_smooth, 1, 0, 0)
        dst_time = join(dst_smooth, other_smooth, time_part)
        src_mask, dst_mask = 2, 1
        while src_mask < src_size or dst_mask < dst_size:
            if src_mask > 2:
                src_time = jnp.concatenate([src_sum, dst_time[rank:]], 0)
                both = src_mask < src_size and dst_mask < dst_size
                add_time = exchanged(dst_time[rank:], src_mask, dst_mask, 0) if both else 0.0
            src_sum = src_time[:src_top]
            add_dst = 0.0
            if dst_mask < dst_size:
                other = exchanged(src_time, 0, dst_mask, 0)
                src_sum, add_time = src_sum + other[:src_top], add_time + other[src_top:]
            if src_mask < src_size:
                other = exchanged(dst_time, src_mask, 0, 0)
                add_dst, add_time = other[:rank], add_time + other[rank:]
            dst_time = jnp.concatenate([dst_time[:rank] + add_dst, dst_time[rank:] + add_time], 0)
            src_mask, dst_mask = src_mask * 2, dst_mask * 2
        grad_src = unpacked(src_sum, rank) / rank
        grad_dst = dst_time[:rank] / rank
        grad_time = dst_time[rank:] / rank
        if iteration + 1 < STEPS:
            src_now = src_now - step_rate * grad_src
            dst_now = dst_now - step_rate * grad_dst
            time_now = time_now - step_rate * grad_time
    return (grad_src, grad_dst.T, grad_time.T)


def solution(mesh):
    in_specs = (P("src", "dst", "tm"), P("src", None), P("dst", None), P("tm", None))
    out_specs = (P("src", None), P("dst", None), P("tm", None))
    return jax.shard_map(
        on_device, mesh=mesh, in_specs=in_specs, out_specs=out_specs, check_vma=False
    )
```
